32 devices in a mesh: groups: 2 (over x), shot: 16 (over z, y, core).
Axes of the slice: x: 2, y: 2, z: 4, core: 2. Of those that a mesh axis runs over, the one named last changes fastest.
Arguments:
- forward_state: float32 [32, 13, 16, 64, 128], P(('groups', 'shot')), parts along dimension 0, may hold values from -6 to 6
- adjoint_state: float32 [32, 13, 16, 64, 128], P(('groups', 'shot')), parts along dimension 0, may hold values from -6 to 6
- source_amp: float32 [32, 2], P(('groups', 'shot')), parts along dimension 0, may hold values from -12 to 12
- source_cell: int32 [32], P(('groups', 'shot')), parts along dimension 0, may hold values from 0 to 131071
- receiver_cells: int32 [32, 1024], P(('groups', 'shot')), parts along dimension 0, may hold values from 0 to 131071
- recorded: float32 [32, 1024], P(('groups', 'shot')), parts along dimension 0, may hold values from -6 to 6
- material: float32 [4, 32, 64, 128], P(None, 'groups', 'shot'), parts along dimension 1, may hold values from 0.3 to 2
- cell_class: int32 [32, 64, 128], P('groups'), parts along dimension 0, may hold values from 0 to 3
- class_factors: float32 [4, 4], replicated, may hold values from 0.5 to 2
Outputs:
- gradient: float32 [4, 32, 64, 128], P(None, 'groups', 'shot'), parts along dimension 1
The draws below stay inside these ranges and needn't reach their ends.
There are 2 independent parts, one for each index of `groups`. The reference program is written for one: setup_inputs(seed, part) draws one part's arguments, and reference() takes and returns one part's arrays. A program takes and returns all parts, laid end to end along the dimension named above; an argument that names none is the same for every part. Nothing has to cross between parts.
All inputs are finite; a program needn't handle non-finite values.
Results may differ from the reference program's by a relative error of at most 0.00002.
Values sent between devices are 32-bit elements; how exact they have to be, the bound alone decides.
A program may use at most 128 MiB of HBM per device.

```python
import math
import jax
import jax.numpy as jnp
from jax import lax

PLANES = 16
NZ = 64
NY = 128
NREC = 1024
NCLASS = 4
SHOTS = 16
CELLS = 131072


def with_ends(drawn, rng, low, top_value):
    index_at = [jax.random.randint(jax.random.fold_in(rng, axis), (), 0, length) for axis, length in enumerate(drawn.shape)]
    longest = drawn.shape.index(max(drawn.shape))
    neighbour = index_at[:longest] + [(index_at[longest] + 1) % drawn.shape[longest]] + index_at[longest + 1:]
    return drawn.at[tuple(index_at)].set(low).at[tuple(neighbour)].set(top_value)


def block_levels(key, extent, cuts, least, high):
    factor_of, own = 1.0, jax.random.fold_in(key, 6)
    for position, blocks in cuts:
        draws = jnp.exp(jax.random.uniform(jax.random.fold_in(own, position), (blocks,), jnp.float32, least / len(cuts), high / len(cuts)))
        factor_of = factor_of * jnp.repeat(draws, extent[position] // blocks).reshape([-1 if axis == position else 1 for axis in range(len(extent))])
    return factor_of


def gaussian(key, dims, scale, reach, cuts=(), held_as=jnp.bfloat16):
    result = scale * jax.random.normal(key, dims, jnp.float32)
    if cuts:
        result = result * block_levels(key, dims, cuts, -0.22, 0.18)
    return jnp.clip(result, -reach, reach).astype(held_as)


def setup_inputs(seed: int = 0, part: int = 0) -> dict:
    seeds = jax.random.split(jax.random.key(seed), 10)
    part_keys = jax.random.split(jax.random.fold_in(seeds[9], part), 10)
    return {
        "forward_state": gaussian(part_keys[0], (SHOTS, 13, PLANES, NZ, NY), 1.0, 6.0, ((0, 16),), jnp.float32),
        "adjoint_state": gaussian(part_keys[1], (SHOTS, 13, PLANES, NZ, NY), 1.0, 6.0, ((0, 16),), jnp.float32),
        "source_amp": gaussian(part_keys[2], (SHOTS, 2), 3.0, 12.0, ((0, 16),), jnp.float32),
        "source_cell": with_ends(jax.random.randint(part_keys[3], (SHOTS,), 0, CELLS), jax.random.fold_in(part_keys[3], 1), 0, CELLS - 1).astype(jnp.int32),
        "receiver_cells": with_ends(jax.random.randint(part_keys[4], (SHOTS, NREC), 0, CELLS), jax.random.fold_in(part_keys[4], 1), 0, CELLS - 1).astype(jnp.int32),
        "recorded": gaussian(part_keys[5], (SHOTS, NREC), 1.0, 6.0, ((0, 16),), jnp.float32),
        "material": jnp.clip(jnp.exp(math.log(2.0) - 1.89712 * jax.random.uniform(part_keys[6], (4, PLANES, NZ, NY), jnp.float32) ** block_levels(part_keys[6], (4, PLANES, NZ, NY), ((2, 16),), -0.2, 0.2)), 0.3, 2.0),
        "cell_class": with_ends(jax.random.randint(part_keys[7], (PLANES, NZ, NY), 0, NCLASS), jax.random.fold_in(part_keys[7], 1), 0, NCLASS - 1).astype(jnp.int32),
        "class_factors": jnp.clip(jnp.exp(jax.random.uniform(seeds[8], (4, NCLASS), jnp.float32, math.log(0.5), math.log(2.0))), 0.5, 2.0),
    }


BIOT_COEFF = 0.8
RHO_BULK = 2.2
RHO_FLUID = 1.0
MASS_FLUID = 2.5
TIME_STEP = 0.25

def forward_diff(field, axis):
    count = field.shape[axis]
    ahead = jnp.concatenate([lax.slice_in_dim(field, 1, count, axis=axis), jnp.zeros_like(lax.slice_in_dim(field, 0, 1, axis=axis))], axis=axis)
    return ahead - field

def backward_diff(field, axis):
    count = field.shape[axis]
    behind = jnp.concatenate([jnp.zeros_like(lax.slice_in_dim(field, 0, 1, axis=axis)), lax.slice_in_dim(field, 0, count - 1, axis=axis)], axis=axis)
    return field - behind

def advance(state, model, amplitude, source):
    vel_x, vel_z, vel_y, flux_x, flux_z, flux_y = (state[0], state[1], state[2], state[3], state[4], state[5])
    sig_xx, sig_zz, sig_yy, sig_xz, sig_xy, sig_zy, pressure = (state[6], state[7], state[8], state[9], state[10], state[11], state[12])
    lame_first, shear_mod, biot_mod, damping = (model[0], model[1], model[2], model[3])
    determinant = RHO_BULK * MASS_FLUID - RHO_FLUID * RHO_FLUID
    force_x = forward_diff(sig_xx, 0) + backward_diff(sig_xz, 1) + backward_diff(sig_xy, 2)
    force_z = backward_diff(sig_xz, 0) + forward_diff(sig_zz, 1) + backward_diff(sig_zy, 2)
    force_y = backward_diff(sig_xy, 0) + backward_diff(sig_zy, 1) + forward_diff(sig_yy, 2)
    drag_x = -forward_diff(pressure, 0) - damping * flux_x
    drag_z = -forward_diff(pressure, 1) - damping * flux_z
    drag_y = -forward_diff(pressure, 2) - damping * flux_y
    vel_x = vel_x + TIME_STEP * (MASS_FLUID * force_x - RHO_FLUID * drag_x) / determinant
    vel_z = vel_z + TIME_STEP * (MASS_FLUID * force_z - RHO_FLUID * drag_z) / determinant
    vel_y = vel_y + TIME_STEP * (MASS_FLUID * force_y - RHO_FLUID * drag_y) / determinant
    flux_x = flux_x + TIME_STEP * (RHO_BULK * drag_x - RHO_FLUID * force_x) / determinant
    flux_z = flux_z + TIME_STEP * (RHO_BULK * drag_z - RHO_FLUID * force_z) / determinant
    flux_y = flux_y + TIME_STEP * (RHO_BULK * drag_y - RHO_FLUID * force_y) / determinant
    strain_xx = backward_diff(vel_x, 0)
    strain_zz = backward_diff(vel_z, 1)
    strain_yy = backward_diff(vel_y, 2)
    div_solid = strain_xx + strain_zz + strain_yy
    div_flux = backward_diff(flux_x, 0) + backward_diff(flux_z, 1) + backward_diff(flux_y, 2)
    strain_xz = 0.5 * (forward_diff(vel_x, 1) + forward_diff(vel_z, 0))
    strain_xy = 0.5 * (forward_diff(vel_x, 2) + forward_diff(vel_y, 0))
    strain_zy = 0.5 * (forward_diff(vel_z, 2) + forward_diff(vel_y, 1))
    bulk_term = (lame_first + BIOT_COEFF * BIOT_COEFF * biot_mod) * div_solid + BIOT_COEFF * biot_mod * div_flux
    sig_xx = sig_xx + TIME_STEP * (2.0 * shear_mod * strain_xx + bulk_term)
    sig_zz = sig_zz + TIME_STEP * (2.0 * shear_mod * strain_zz + bulk_term)
    sig_yy = sig_yy + TIME_STEP * (2.0 * shear_mod * strain_yy + bulk_term)
    sig_xz = sig_xz + TIME_STEP * 2.0 * shear_mod * strain_xz
    sig_xy = sig_xy + TIME_STEP * 2.0 * shear_mod * strain_xy
    sig_zy = sig_zy + TIME_STEP * 2.0 * shear_mod * strain_zy
    pressure = pressure - TIME_STEP * biot_mod * (BIOT_COEFF * div_solid + div_flux)
    pressure = pressure.reshape(-1).at[source].add(amplitude).reshape(pressure.shape)
    return jnp.stack([vel_x, vel_z, vel_y, flux_x, flux_z, flux_y, sig_xx, sig_zz, sig_yy, sig_xz, sig_xy, sig_zy, pressure])

def shot_gradient(model, start_state, adjoint, amplitudes, source, receivers, observed):

    def march(params):
        state = start_state
        for section in range(2):
            state = advance(state, params, amplitudes[section], source)
        return state
    final, pullback = jax.vjp(march, model)
    misfit = final[12].reshape(-1)[receivers] - observed
    pressure_cot = adjoint[12].reshape(-1).at[receivers].add(misfit).reshape(adjoint[12].shape)
    cotangent = adjoint.at[12].set(pressure_cot)
    return pullback(cotangent)[0]

def class_factor_map(cell_class, class_factors):
    classes = jnp.arange(class_factors.shape[1], dtype=jnp.int32)
    onehot = (cell_class[None] == classes[:, None, None, None]).astype(jnp.float32)
    return lax.optimization_barrier(jnp.sum(class_factors[:, :, None, None, None] * onehot[None], axis=1))

def reference(forward_state, adjoint_state, source_amp, source_cell, receiver_cells, recorded, material, cell_class, class_factors):
    factor = class_factor_map(cell_class, class_factors)
    model = material * factor

    def accumulate(total, items):
        start_state, adjoint, amplitudes, source, receivers, observed = items
        return (total + shot_gradient(model, start_state, adjoint, amplitudes, source, receivers, observed), None)
    total, unused = lax.scan(accumulate, jnp.zeros_like(material), (forward_state, adjoint_state, source_amp, source_cell, receiver_cells, recorded))
    return total * factor / jnp.sqrt(jnp.float32(SHOTS))
```

```python
import functools

import jax
import jax.numpy as jnp
from jax import lax
from jax.experimental import pallas as pl
from jax.experimental.pallas import tpu as pltpu
from jax.sharding import PartitionSpec as P

BIOT_COEFF = 0.8
RHO_BULK = 2.2
RHO_FLUID = 1.0
MASS_FLUID = 2.5
TIME_STEP = 0.25
DET = RHO_BULK * MASS_FLUID - RHO_FLUID * RHO_FLUID
C_M = TIME_STEP * MASS_FLUID / DET
C_A = TIME_STEP * RHO_BULK / DET
C_B = TIME_STEP * RHO_FLUID / DET

VX, VZ, VY, QX, QZ, QY, SXX, SZZ, SYY, SXZ, SXY, SZY, PR = range(13)
MESH = pl.DeviceIdType.MESH
F32 = jnp.float32


def coordinates(n):
    me = lax.axis_index("shot")
    return me, lax.rem(me, 2), lax.rem(me // 2, 2), me // 4, n // 4


def index_of(z, y, core):
    return (z * 2 + y) * 2 + core


def greet(n):
    me, core, y, z, zs = coordinates(n)
    barrier = pltpu.get_barrier_semaphore()
    peers = [index_of(z, y, 1 - core), index_of(z, 1 - y, core)]
    peers += [index_of(lax.rem(z + d, zs), y, core) for d in range(1, zs)]
    for peer in peers:
        pl.semaphore_signal(barrier, inc=1, device_id={"shot": peer}, device_id_type=MESH)
    pl.semaphore_wait(barrier, len(peers))


def gather_kernel(n, own_ref, out_ref, local_sem, zs_sem, zr_sem, ys_sem, yr_sem, cs_sem, cr_sem):
    me, core, y, z, zs = coordinates(n)
    other_core = {"shot": index_of(z, y, 1 - core)}
    other_side = {"shot": index_of(z, 1 - y, core)}
    mine = pltpu.make_async_copy(own_ref, out_ref.at[me], local_sem)
    mine.start()
    greet(n)

    def send(src, slot, send_sem, recv_sem, target):
        copy = pltpu.make_async_remote_copy(
            src_ref=src, dst_ref=out_ref.at[slot], send_sem=send_sem, recv_sem=recv_sem,
            device_id=target, device_id_type=MESH)
        copy.start()
        return copy

    along, across, inside = [], [], []
    across.append(send(own_ref, me, ys_sem.at[0], yr_sem.at[0], other_side))
    for d in range(1, zs):
        target = {"shot": index_of(lax.rem(z + d, zs), y, core)}
        along.append(send(own_ref, me, zs_sem.at[d], zr_sem.at[d], target))
    inside.append(send(own_ref, me, cs_sem.at[0], cr_sem.at[0], other_core))
    for d in range(1, zs):
        along[d - 1].wait_recv()
        slot = index_of(lax.rem(z + zs - d, zs), y, core)
        across.append(send(out_ref.at[slot], slot, ys_sem.at[d], yr_sem.at[d], other_side))
        inside.append(send(out_ref.at[slot], slot, cs_sem.at[d], cr_sem.at[d], other_core))
    for d in range(zs):
        across[d].wait_recv()
        slot = index_of(lax.rem(z + zs - d, zs), 1 - y, core)
        inside.append(send(out_ref.at[slot], slot, cs_sem.at[zs + d], cr_sem.at[zs + d], other_core))
    for copy in inside:
        copy.wait_recv()
    for copy in along + across + inside:
        copy.wait_send()
    mine.wait()


def gather_slabs(own, n):
    zs = n // 4
    dma = pltpu.SemaphoreType.DMA
    return pl.pallas_call(
        functools.partial(gather_kernel, n),
        out_shape=jax.ShapeDtypeStruct((n,) + own.shape, own.dtype),
        in_specs=[pl.BlockSpec(memory_space=pltpu.VMEM)],
        out_specs=pl.BlockSpec(memory_space=pltpu.VMEM),
        scratch_shapes=[dma, dma((zs,)), dma((zs,)), dma((zs,)), dma((zs,)), dma((2 * zs,)), dma((2 * zs,))],
        compiler_params=pltpu.CompilerParams(collective_id=0, has_side_effects=True, vmem_limit_bytes=8 << 20),
        name="gather_slabs",
    )(own)


def scatter_kernel(n, term_ref, out_ref, from_core, to_side, from_side, to_line, from_line,
                   cs_sem, cr_sem, ys_sem, yr_sem, zs_sem, zr_sem):
    me, core, y, z, zs = coordinates(n)
    other_core = {"shot": index_of(z, y, 1 - core)}
    other_side = {"shot": index_of(z, 1 - y, core)}
    greet(n)

    def send(src, dst, send_sem, recv_sem, target):
        copy = pltpu.make_async_remote_copy(
            src_ref=src, dst_ref=dst, send_sem=send_sem, recv_sem=recv_sem,
            device_id=target, device_id_type=MESH)
        copy.start()
        return copy

    order = list(range(1, zs)) + [0]
    place = {d: lax.rem(z + d, zs) for d in order}
    inside, across, along = {}, {}, {}
    for far in (1, 0):
        side = 1 - y if far else y
        for d in order:
            k = far * zs + d
            inside[k] = send(term_ref.at[index_of(place[d], side, 1 - core)], from_core.at[k],
                             cs_sem.at[k], cr_sem.at[k], other_core)
    for d in order:
        inside[zs + d].wait_recv()
        to_side[d] = term_ref[index_of(place[d], 1 - y, core)] + from_core[zs + d]
        across[d] = send(to_side.at[d], from_side.at[d], ys_sem.at[d], yr_sem.at[d], other_side)
    for d in order:
        inside[d].wait_recv()
        across[d].wait_recv()
        total = term_ref[index_of(place[d], y, core)] + from_core[d] + from_side[d]
        to_line[d] = total
        if d:
            target = {"shot": index_of(place[d], y, core)}
            along[d] = send(to_line.at[d], from_line.at[d], zs_sem.at[d], zr_sem.at[d], target)
    result = to_line[0]
    for d in range(1, zs):
        along[d].wait_recv()
        result = result + from_line[d]
    out_ref[...] = result
    for copies in (inside, across, along):
        for copy in copies.values():
            copy.wait_send()


def scatter_slabs(terms):
    n, slab = terms.shape[0], terms.shape[1:]
    zs = n // 4
    dma = pltpu.SemaphoreType.DMA
    return pl.pallas_call(
        functools.partial(scatter_kernel, n),
        out_shape=jax.ShapeDtypeStruct(slab, terms.dtype),
        in_specs=[pl.BlockSpec(memory_space=pltpu.VMEM)],
        out_specs=pl.BlockSpec(memory_space=pltpu.VMEM),
        scratch_shapes=[
            pltpu.VMEM((2 * zs,) + slab, F32),
            pltpu.VMEM((zs,) + slab, F32), pltpu.VMEM((zs,) + slab, F32),
            pltpu.VMEM((zs,) + slab, F32), pltpu.VMEM((zs,) + slab, F32),
            dma((2 * zs,)), dma((2 * zs,)), dma((zs,)), dma((zs,)), dma((zs,)), dma((zs,))],
        compiler_params=pltpu.CompilerParams(collective_id=1, has_side_effects=True, vmem_limit_bytes=16 << 20),
        name="scatter_slabs",
    )(terms)


class Window:
    def __init__(self, x, z0, zc, nz, ny):
        self.x, self.z0, self.zc, self.nz = x, z0, zc, nz
        self.row = lax.broadcasted_iota(jnp.int32, (zc, ny), 0)
        self.lane = lax.broadcasted_iota(jnp.int32, (zc, ny), 1)
        self.ny = ny
        self.seen = {}

    def at(self, ref, f, dx=0, dz=0):
        key = (id(ref), f, dx, dz)
        if key in self.seen:
            return self.seen[key]
        plane = self.x + 1 + dx
        lo = self.z0 + dz
        if lo < 0:
            value = self.at(ref, f, dx)
            value = jnp.where(self.row == 0, 0.0, pltpu.roll(value, 1, 0))
        elif lo + self.zc > self.nz:
            value = self.at(ref, f, dx)
            value = jnp.where(self.row == self.zc - 1, 0.0, pltpu.roll(value, self.zc - 1, 0))
        else:
            value = ref[f, plane, lo:lo + self.zc, :]
        self.seen[key] = value
        return value

    def fx(self, ref, f):
        return self.at(ref, f, 1) - self.at(ref, f)

    def bx(self, ref, f):
        return self.at(ref, f) - self.at(ref, f, -1)

    def fz(self, ref, f):
        return self.at(ref, f, 0, 1) - self.at(ref, f)

    def bz(self, ref, f):
        return self.at(ref, f) - self.at(ref, f, 0, -1)

    def fy(self, ref, f):
        value = self.at(ref, f)
        return jnp.where(self.lane == self.ny - 1, 0.0, pltpu.roll(value, self.ny - 1, 1)) - value

    def by(self, ref, f):
        value = self.at(ref, f)
        return value - jnp.where(self.lane == 0, 0.0, pltpu.roll(value, 1, 1))

    def put(self, ref, f, value):
        ref[f, self.x + 1, self.z0:self.z0 + self.zc, :] = value


def shot_kernel(n, zc, fwd_hbm, adj_hbm, amp_ref, src_ref, rec_ref, obs_ref, gathered_ref, class_ref, cf_ref,
                out_ref, st, ad, q1, q2, e1, be, bf, mat, grad, cnt, obs, fwd_sem, adj_sem):
    planes, nz, ny = class_ref.shape
    piece = gathered_ref.shape[2]
    classes = cf_ref.shape[1]

    def fwd_copy(x):
        return pltpu.make_async_copy(fwd_hbm.at[:, x], st.at[:, x + 1], fwd_sem.at[x])

    def adj_copy(x):
        return pltpu.make_async_copy(adj_hbm.at[:, x], ad.at[:, x + 1], adj_sem.at[x])

    for x in range(planes):
        fwd_copy(x).start()
    for x in range(planes):
        adj_copy(x).start()

    zero_plane = jnp.zeros((nz, ny), F32)
    for ref in (st, q1, q2, be, bf):
        for f in range(ref.shape[0]):
            ref[f, 0] = zero_plane
            ref[f, planes + 1] = zero_plane

    cells = rec_ref[...]
    rows = lax.div(cells, jnp.int32(ny))
    lanes = cells - rows * ny
    count = cells.shape[1]
    value = obs_ref[...]
    hi = value.astype(jnp.bfloat16).astype(F32)
    mid = (value - hi).astype(jnp.bfloat16).astype(F32)
    low = value - hi - mid
    hit = lax.broadcasted_iota(jnp.int32, (ny, count), 0) == lanes
    columns = jnp.concatenate(
        [jnp.where(hit, part, 0.0).astype(jnp.bfloat16) for part in (jnp.ones_like(value), hi, mid, low)], axis=0)

    def place_receivers(x, carry):
        at_row = lax.broadcasted_iota(jnp.int32, (nz, count), 0) + x * nz == rows
        product = lax.dot_general(
            jnp.where(at_row, 1.0, 0.0).astype(jnp.bfloat16), columns, (((1,), (1,)), ((), ())),
            preferred_element_type=F32)
        cnt[x] = product[:, :ny]
        obs[x] = product[:, ny:2 * ny] + product[:, 2 * ny:3 * ny] + product[:, 3 * ny:]
        return carry

    lax.fori_loop(0, planes, place_receivers, 0)

    def factor_of(k, cls):
        factor = jnp.full(cls.shape, cf_ref[k, classes - 1], F32)
        for c in range(classes - 1):
            factor = jnp.where(cls == c, cf_ref[k, c], factor)
        return factor

    scales = (TIME_STEP, 2.0 * TIME_STEP, TIME_STEP, 1.0)

    def build_model(x, carry):
        cls = class_ref[x]
        for k in range(4):
            for d in range(n):
                mat[k, x + 1, d * piece:(d + 1) * piece, :] = gathered_ref[d, k * planes + x]
            mat[k, x + 1] = mat[k, x + 1] * factor_of(k, cls) * scales[k]
        return carry

    lax.fori_loop(0, planes, build_model, 0)

    source = src_ref[0]
    L, U, B, D = range(4)

    def sweep(body, before=None):
        def plane(x, carry):
            if before is not None:
                before(x)
            for z0 in range(0, nz, zc):
                body(Window(x, z0, zc, nz, ny))
            return carry
        lax.fori_loop(0, planes, plane, 0)

    def velocities(q_old, base, q_new, w):
        damp = w.at(mat, D)
        forces = (
            w.fx(st, SXX) + w.bz(st, SXZ) + w.by(st, SXY),
            w.bx(st, SXZ) + w.fz(st, SZZ) + w.by(st, SZY),
            w.bx(st, SXY) + w.bz(st, SZY) + w.fy(st, SYY))
        slopes = (w.fx(st, PR), w.fz(st, PR), w.fy(st, PR))
        for i in range(3):
            flux = w.at(q_old, base + i)
            pull = slopes[i] + damp * flux
            w.put(st, VX + i, w.at(st, VX + i) + (C_M * forces[i] + C_B * pull))
            w.put(q_new, i, flux - (C_A * pull + C_B * forces[i]))

    def strains(q, w):
        exx, ezz, eyy = w.bx(st, VX), w.bz(st, VZ), w.by(st, VY)
        dv = exx + ezz + eyy
        g = BIOT_COEFF * dv + (w.bx(q, 0) + w.bz(q, 1) + w.by(q, 2))
        gxz = w.fz(st, VX) + w.fx(st, VZ)
        gxy = w.fy(st, VX) + w.fx(st, VY)
        gzy = w.fy(st, VZ) + w.fz(st, VY)
        return exx, ezz, eyy, gxz, gxy, gzy, dv, g

    def add_source(w, section, pressure):
        here = (w.row + (w.x * nz + w.z0)) * ny + w.lane == source
        return pressure + jnp.where(here, amp_ref[0, section], 0.0)

    def correlate(w, bars, bar_p, terms):
        exx, ezz, eyy, gxz, gxy, gzy, dv, g = terms
        trace = bars[0] + bars[1] + bars[2]
        aside = BIOT_COEFF * trace - bar_p
        g_lame = trace * dv
        g_shear = 2.0 * (bars[0] * exx + bars[1] * ezz + bars[2] * eyy) + (
            bars[3] * gxz + bars[4] * gxy + bars[5] * gzy)
        g_biot = g * aside
        h = w.at(mat, B) * aside
        common = w.at(mat, L) * trace + BIOT_COEFF * h
        shear2 = w.at(mat, U)
        shear1 = 0.5 * shear2
        for i in range(3):
            w.put(be, i, shear2 * bars[i] + common)
            w.put(be, 3 + i, shear1 * bars[3 + i])
        w.put(be, 6, h)
        return g_lame, g_shear, g_biot

    def bar_motion(w):
        vels = (
            w.at(ad, VX) - (w.fx(be, 0) + w.bz(be, 3) + w.by(be, 4)),
            w.at(ad, VZ) - (w.fz(be, 1) + w.bx(be, 3) + w.by(be, 5)),
            w.at(ad, VY) - (w.fy(be, 2) + w.bx(be, 4) + w.bz(be, 5)))
        fluxes = (
            w.at(ad, QX) - w.fx(be, 6), w.at(ad, QZ) - w.fz(be, 6), w.at(ad, QY) - w.fy(be, 6))
        return vels, fluxes

    def rows_of(ref, k, w):
        return ref[k, w.x, w.z0:w.z0 + zc, :]

    fwd_copy(0).wait()

    def next_forward(x):
        @pl.when(x + 1 < planes)
        def _():
            fwd_copy(x + 1).wait()

    sweep(functools.partial(velocities, st, QX, q1), next_forward)

    def stresses(w):
        terms = strains(q1, w)
        exx, ezz, eyy, gxz, gxy, gzy, dv, g = terms
        bg = w.at(mat, B) * g
        bulk = w.at(mat, L) * dv + BIOT_COEFF * bg
        shear2 = w.at(mat, U)
        shear1 = 0.5 * shear2
        for i, e in enumerate((exx, ezz, eyy)):
            w.put(st, SXX + i, w.at(st, SXX + i) + (shear2 * e + bulk))
        for i, e in enumerate((gxz, gxy, gzy)):
            w.put(st, SXZ + i, w.at(st, SXZ + i) + shear1 * e)
        w.put(st, PR, add_source(w, 0, w.at(st, PR) - bg))
        for i, e in enumerate((exx, ezz, eyy, gxz, gxy, gzy, g)):
            e1[i, w.x, w.z0:w.z0 + zc, :] = e

    sweep(stresses)

    sweep(functools.partial(velocities, q1, 0, q2))

    def turn(w):
        terms = strains(q2, w)
        final = add_source(w, 1, w.at(st, PR) - w.at(mat, B) * terms[7])
        here = slice(w.z0, w.z0 + zc)
        bar_p = w.at(ad, PR) + (cnt[w.x, here, :] * final - obs[w.x, here, :])
        w.put(ad, PR, bar_p)
        parts = correlate(w, [w.at(ad, SXX + i) for i in range(6)], bar_p, terms)
        for k in range(3):
            grad[k, w.x, here, :] = parts[k]

    sweep(turn, lambda x: adj_copy(x).wait())

    def back_motion(w):
        vels, fluxes = bar_motion(w)
        damp = w.at(mat, D)
        total = None
        for i in range(3):
            bar_f = C_M * vels[i] - C_B * fluxes[i]
            bar_r = C_A * fluxes[i] - C_B * vels[i]
            w.put(bf, i, bar_f)
            w.put(bf, 3 + i, bar_r)
            part = w.at(q1, i) * bar_r
            total = part if total is None else total + part
            w.put(ad, VX + i, vels[i])
            w.put(ad, QX + i, fluxes[i] - damp * bar_r)
        grad[3, w.x, w.z0:w.z0 + zc, :] = total

    sweep(back_motion)

    def back_stress(w):
        bars = (
            w.at(ad, SXX) - w.bx(bf, 0),
            w.at(ad, SZZ) - w.bz(bf, 1),
            w.at(ad, SYY) - w.by(bf, 2),
            w.at(ad, SXZ) - (w.fz(bf, 0) + w.fx(bf, 1)),
            w.at(ad, SXY) - (w.fy(bf, 0) + w.fx(bf, 2)),
            w.at(ad, SZY) - (w.fy(bf, 1) + w.fz(bf, 2)))
        bar_p = w.at(ad, PR) + (w.bx(bf, 3) + w.bz(bf, 4) + w.by(bf, 5))
        terms = [rows_of(e1, i, w) for i in range(6)]
        terms += [terms[0] + terms[1] + terms[2], rows_of(e1, 6, w)]
        parts = correlate(w, bars, bar_p, terms)
        for k in range(3):
            grad[k, w.x, w.z0:w.z0 + zc, :] = rows_of(grad, k, w) + parts[k]

    sweep(back_stress)

    root = float(n) ** 0.5
    signs = (TIME_STEP / root, TIME_STEP / root, TIME_STEP / root, -1.0 / root)

    def finish(w):
        vels, fluxes = bar_motion(w)
        damp = rows_of(grad, 3, w)
        for i in range(3):
            damp = damp + w.at(st, QX + i) * (C_A * fluxes[i] - C_B * vels[i])
        cls = class_ref[w.x, w.z0:w.z0 + zc, :]
        for k in range(4):
            total = damp if k == 3 else rows_of(grad, k, w)
            total = total * (factor_of(k, cls) * signs[k])
            for r in range(0, zc, piece):
                out_ref[(w.z0 + r) // piece, k * planes + w.x] = total[r:r + piece]

    sweep(finish)


def shot_terms(forward, adjoint, amplitudes, source, receivers, observed, gathered, cell_class, class_factors, n):
    fields, planes, nz, ny = forward.shape
    vmem = pl.BlockSpec(memory_space=pltpu.VMEM)
    smem = pl.BlockSpec(memory_space=pltpu.SMEM)
    hbm = pl.BlockSpec(memory_space=pl.ANY)
    padded = lambda f: pltpu.VMEM((f, planes + 2, nz, ny), F32)
    plain = lambda f: pltpu.VMEM((f, planes, nz, ny), F32)
    return pl.pallas_call(
        functools.partial(shot_kernel, n, 8),
        out_shape=jax.ShapeDtypeStruct(gathered.shape, F32),
        in_specs=[hbm, hbm, smem, smem, vmem, vmem, vmem, vmem, smem],
        out_specs=vmem,
        scratch_shapes=[
            padded(fields), padded(fields), padded(3), padded(3), plain(7), padded(7), padded(6), padded(4), plain(4),
            pltpu.VMEM((planes, nz, ny), F32), pltpu.VMEM((planes, nz, ny), F32),
            pltpu.SemaphoreType.DMA((planes,)), pltpu.SemaphoreType.DMA((planes,))],
        compiler_params=pltpu.CompilerParams(vmem_limit_bytes=48 << 20),
        name="shot_terms",
    )(forward, adjoint, amplitudes, source, receivers, observed, gathered, cell_class, class_factors)


def per_device(forward_state, adjoint_state, source_amp, source_cell, receiver_cells, recorded, material,
               cell_class, class_factors):
    n = lax.axis_size("shot")
    params, planes, piece, ny = material.shape
    gathered = gather_slabs(material.reshape(params * planes, piece, ny), n)
    terms = shot_terms(forward_state[0], adjoint_state[0], source_amp, source_cell, receiver_cells, recorded,
                       gathered, cell_class, class_factors, n)
    return scatter_slabs(terms).reshape(material.shape)


def solution(mesh):
    placed = (
        P(("groups", "shot"), None, None, None, None),
        P(("groups", "shot"), None, None, None, None),
        P(("groups", "shot"), None),
        P(("groups", "shot")),
        P(("groups", "shot"), None),
        P(("groups", "shot"), None),
        P(None, "groups", "shot", None),
        P("groups", None, None),
        P(),
    )
    return jax.shard_map(
        per_device, mesh=mesh, in_specs=placed, out_specs=P(None, "groups", "shot", None), check_vma=False)
```

```python
import functools

import jax
import jax.numpy as jnp
from jax import lax
from jax.experimental import pallas as pl
from jax.experimental.pallas import tpu as pltpu
from jax.sharding import PartitionSpec as P

BIOT_COEFF = 0.8
RHO_BULK = 2.2
RHO_FLUID = 1.0
MASS_FLUID = 2.5
TIME_STEP = 0.25
DET = RHO_BULK * MASS_FLUID - RHO_FLUID * RHO_FLUID
C_M = TIME_STEP * MASS_FLUID / DET
C_A = TIME_STEP * RHO_BULK / DET
C_B = TIME_STEP * RHO_FLUID / DET

VX, VZ, VY, QX, QZ, QY, SXX, SZZ, SYY, SXZ, SXY, SZY, PR = range(13)
MESH = pl.DeviceIdType.MESH
F32 = jnp.float32


def coordinates(n):
    me = lax.axis_index("shot")
    return lax.rem(me, 2), lax.rem(me // 2, 2), me // 4, n // 4


def index_of(z, y, core):
    return (z * 2 + y) * 2 + core


class Window:
    def __init__(self, x, z0, zc, nz, ny):
        self.x, self.z0, self.zc, self.nz = x, z0, zc, nz
        self.row = lax.broadcasted_iota(jnp.int32, (zc, ny), 0)
        self.lane = lax.broadcasted_iota(jnp.int32, (zc, ny), 1)
        self.ny = ny
        self.seen = {}

    def at(self, ref, f, dx=0, dz=0):
        key = (id(ref), f, dx, dz)
        if key in self.seen:
            return self.seen[key]
        plane = self.x + 1 + dx
        lo = self.z0 + dz
        if lo < 0:
            value = self.at(ref, f, dx)
            value = jnp.where(self.row == 0, 0.0, pltpu.roll(value, 1, 0))
        elif lo + self.zc > self.nz:
            value = self.at(ref, f, dx)
            value = jnp.where(self.row == self.zc - 1, 0.0, pltpu.roll(value, self.zc - 1, 0))
        else:
            value = ref[f, plane, lo:lo + self.zc, :]
        self.seen[key] = value
        return value

    def fx(self, ref, f):
        return self.at(ref, f, 1) - self.at(ref, f)

    def bx(self, ref, f):
        return self.at(ref, f) - self.at(ref, f, -1)

    def fz(self, ref, f):
        return self.at(ref, f, 0, 1) - self.at(ref, f)

    def bz(self, ref, f):
        return self.at(ref, f) - self.at(ref, f, 0, -1)

    def fy(self, ref, f):
        value = self.at(ref, f)
        return jnp.where(self.lane == self.ny - 1, 0.0, pltpu.roll(value, self.ny - 1, 1)) - value

    def by(self, ref, f):
        value = self.at(ref, f)
        return value - jnp.where(self.lane == 0, 0.0, pltpu.roll(value, 1, 1))

    def put(self, ref, f, value):
        ref[f, self.x + 1, self.z0:self.z0 + self.zc, :] = value


STAGES = 7


def kernel(n, zc, fwd_hbm, adj_hbm, amp_hbm, src_hbm, rec_hbm, obs_hbm, own_hbm, class_hbm, cf_hbm,
           out_ref, amp_ref, src_ref, rec_ref, obs_in, class_ref, cf_ref, gathered, terms_ref,
           from_core, to_side, from_side, to_line, from_line,
           st, ad, q1, q2, e1, be, bf, mat, grad, cnt, obs,
           fwd_sem, adj_sem, small_sem, own_sem,
           gz_s, gz_r, gy_s, gy_r, gc_s, gc_r, rc_s, rc_r, ry_s, ry_r, rz_s, rz_r):
    planes, nz, ny = class_ref.shape
    chunks, zs = gathered.shape[0], gathered.shape[1]
    per = planes // chunks
    lag = (STAGES - 1) // per
    piece = gathered.shape[6]
    classes = cf_ref.shape[1]
    core, y, z, _ = coordinates(n)
    other_core = {"shot": index_of(z, y, 1 - core)}
    other_side = {"shot": index_of(z, 1 - y, core)}

    def on_line(d):
        return lax.rem(z + d, zs)

    def own_copy(c):
        return pltpu.make_async_copy(own_hbm.at[:, pl.ds(c * per, per)], gathered.at[c, z, y, core], own_sem.at[c])

    def fwd_copy(x):
        return pltpu.make_async_copy(fwd_hbm.at[:, x], st.at[:, x + 1], fwd_sem.at[x])

    def adj_copy(x):
        return pltpu.make_async_copy(adj_hbm.at[:, x], ad.at[:, x + 1], adj_sem.at[x])

    small = [pltpu.make_async_copy(src, dst, small_sem.at[i]) for i, (src, dst) in enumerate((
        (rec_hbm, rec_ref), (obs_hbm, obs_in), (amp_hbm, amp_ref), (src_hbm, src_ref), (cf_hbm, cf_ref),
        (class_hbm, class_ref)))]

    def remote(src, dst, send_sem, recv_sem, target):
        return pltpu.make_async_remote_copy(
            src_ref=src, dst_ref=dst, send_sem=send_sem, recv_sem=recv_sem, device_id=target, device_id_type=MESH)

    def gather_line(c, d):
        slab = gathered.at[c, z, y, core]
        return remote(slab, slab, gz_s.at[d - 1, c], gz_r.at[d - 1, c], {"shot": index_of(on_line(d), y, core)})

    def gather_side(c):
        slabs = gathered.at[c, :, y, core]
        return remote(slabs, slabs, gy_s.at[c], gy_r.at[c], other_side)

    def gather_core(c):
        slabs = gathered.at[c, :, :, core]
        return remote(slabs, slabs, gc_s.at[c], gc_r.at[c], other_core)

    def reduce_core(c):
        return remote(terms_ref.at[c, :, :, 1 - core], from_core.at[c], rc_s.at[c], rc_r.at[c], other_core)

    def reduce_side(c):
        return remote(to_side.at[c], from_side.at[c], ry_s.at[c], ry_r.at[c], other_side)

    def reduce_line(c, d):
        return remote(to_line.at[c, d - 1], from_line.at[c, d - 1], rz_s.at[d - 1, c], rz_r.at[d - 1, c],
                      {"shot": index_of(on_line(d), y, core)})

    def within(c, step):
        @pl.when(jnp.logical_and(c >= 0, c < chunks))
        def _():
            step(c)

    def gather_0(c):
        own_copy(c).wait()
        for d in range(1, zs):
            gather_line(c, d).start()

    def gather_1(c):
        for d in range(1, zs):
            gather_line(c, d).wait_recv()
        gather_side(c).start()

    def gather_2(c):
        gather_side(c).wait_recv()
        gather_core(c).start()

    def gather_3(c):
        gather_core(c).wait_recv()

    def reduce_0(c):
        reduce_core(c).start()

    def reduce_1(c):
        reduce_core(c).wait_recv()
        for s in range(zs):
            to_side[c, s] = terms_ref[c, s, 1 - y, core] + from_core[c, s, 1 - y]
        reduce_side(c).start()

    def reduce_2(c):
        reduce_side(c).wait_recv()
        for d in range(1, zs):
            s = on_line(d)
            to_line[c, d - 1] = terms_ref[c, s, y, core] + from_core[c, s, y] + from_side[c, s]
            reduce_line(c, d).start()

    def reduce_3(c):
        total = terms_ref[c, z, y, core] + from_core[c, z, y] + from_side[c, z]
        for d in range(1, zs):
            reduce_line(c, d).wait_recv()
            total = total + from_line[c, d - 1]
        out_ref[:, pl.ds(c * per, per)] = total

    for c in range(chunks):
        own_copy(c).start()
    for copy in small:
        copy.start()
    for x in range(planes):
        fwd_copy(x).start()
    for x in range(planes):
        adj_copy(x).start()

    barrier = pltpu.get_barrier_semaphore()
    for target in [other_core, other_side] + [{"shot": index_of(on_line(d), y, core)} for d in range(1, zs)]:
        pl.semaphore_signal(barrier, inc=1, device_id=target, device_id_type=MESH)
    zero_plane = jnp.zeros((nz, ny), F32)
    for ref in (st, q1, q2, be, bf):
        for f in range(ref.shape[0]):
            ref[f, 0] = zero_plane
            ref[f, planes + 1] = zero_plane
    pl.semaphore_wait(barrier, zs + 1)

    ahead = min(3, chunks)
    for c in range(ahead):
        gather_0(c)
    for copy in small:
        copy.wait()

    cells = rec_ref[...]
    rows = lax.div(cells, jnp.int32(ny))
    lanes = cells - rows * ny
    count = cells.shape[1]
    value = obs_in[...]
    hi = value.astype(jnp.bfloat16).astype(F32)
    mid = (value - hi).astype(jnp.bfloat16).astype(F32)
    low = value - hi - mid
    hit = lax.broadcasted_iota(jnp.int32, (ny, count), 0) == lanes
    columns = jnp.concatenate(
        [jnp.where(hit, part, 0.0).astype(jnp.bfloat16) for part in (jnp.ones_like(value), hi, mid, low)], axis=0)

    def place_receivers(x, carry):
        at_row = lax.broadcasted_iota(jnp.int32, (nz, count), 0) + x * nz == rows
        product = lax.dot_general(
            jnp.where(at_row, 1.0, 0.0).astype(jnp.bfloat16), columns, (((1,), (1,)), ((), ())),
            preferred_element_type=F32)
        cnt[x] = product[:, :ny]
        obs[x] = product[:, ny:2 * ny] + product[:, 2 * ny:3 * ny] + product[:, 3 * ny:]
        return carry

    gather_1(0)
    lax.fori_loop(0, planes, place_receivers, 0)
    gather_2(0)
    if chunks > 1:
        gather_1(1)

    def factor_of(k, cls):
        factor = jnp.full(cls.shape, cf_ref[k, classes - 1], F32)
        for c in range(classes - 1):
            factor = jnp.where(cls == c, cf_ref[k, c], factor)
        return factor

    scales = (TIME_STEP, 2.0 * TIME_STEP, TIME_STEP, 1.0)

    source = src_ref[0]
    L, U, B, D = range(4)

    def velocities(q_old, base, q_new, w):
        damp = w.at(mat, D)
        forces = (
            w.fx(st, SXX) + w.bz(st, SXZ) + w.by(st, SXY),
            w.bx(st, SXZ) + w.fz(st, SZZ) + w.by(st, SZY),
            w.bx(st, SXY) + w.bz(st, SZY) + w.fy(st, SYY))
        slopes = (w.fx(st, PR), w.fz(st, PR), w.fy(st, PR))
        for i in range(3):
            flux = w.at(q_old, base + i)
            pull = slopes[i] + damp * flux
            w.put(st, VX + i, w.at(st, VX + i) + (C_M * forces[i] + C_B * pull))
            w.put(q_new, i, flux - (C_A * pull + C_B * forces[i]))

    def strains(q, w):
        exx, ezz, eyy = w.bx(st, VX), w.bz(st, VZ), w.by(st, VY)
        dv = exx + ezz + eyy
        g = BIOT_COEFF * dv + (w.bx(q, 0) + w.bz(q, 1) + w.by(q, 2))
        gxz = w.fz(st, VX) + w.fx(st, VZ)
        gxy = w.fy(st, VX) + w.fx(st, VY)
        gzy = w.fy(st, VZ) + w.fz(st, VY)
        return exx, ezz, eyy, gxz, gxy, gzy, dv, g

    def add_source(w, section, pressure):
        here = (w.row + (w.x * nz + w.z0)) * ny + w.lane == source
        return pressure + jnp.where(here, amp_ref[0, section], 0.0)

    def correlate(w, bars, bar_p, terms):
        exx, ezz, eyy, gxz, gxy, gzy, dv, g = terms
        trace = bars[0] + bars[1] + bars[2]
        aside = BIOT_COEFF * trace - bar_p
        g_lame = trace * dv
        g_shear = 2.0 * (bars[0] * exx + bars[1] * ezz + bars[2] * eyy) + (
            bars[3] * gxz + bars[4] * gxy + bars[5] * gzy)
        g_biot = g * aside
        h = w.at(mat, B) * aside
        common = w.at(mat, L) * trace + BIOT_COEFF * h
        shear2 = w.at(mat, U)
        shear1 = 0.5 * shear2
        for i in range(3):
            w.put(be, i, shear2 * bars[i] + common)
            w.put(be, 3 + i, shear1 * bars[3 + i])
        w.put(be, 6, h)
        return g_lame, g_shear, g_biot

    def bar_motion(w):
        vels = (
            w.at(ad, VX) - (w.fx(be, 0) + w.bz(be, 3) + w.by(be, 4)),
            w.at(ad, VZ) - (w.fz(be, 1) + w.bx(be, 3) + w.by(be, 5)),
            w.at(ad, VY) - (w.fy(be, 2) + w.bx(be, 4) + w.bz(be, 5)))
        fluxes = (
            w.at(ad, QX) - w.fx(be, 6), w.at(ad, QZ) - w.fz(be, 6), w.at(ad, QY) - w.fy(be, 6))
        return vels, fluxes

    def rows_of(ref, k, w):
        return ref[k, w.x, w.z0:w.z0 + zc, :]


    def build_plane(c, j, x):
        cls = class_ref[x]
        for k in range(4):
            for d in range(n):
                mat[k, x + 1, d * piece:(d + 1) * piece, :] = gathered[c, d // 4, d // 2 % 2, d % 2, k, j]
            mat[k, x + 1] = mat[k, x + 1] * factor_of(k, cls) * scales[k]

    def stresses(w):
        terms = strains(q1, w)
        exx, ezz, eyy, gxz, gxy, gzy, dv, g = terms
        bg = w.at(mat, B) * g
        bulk = w.at(mat, L) * dv + BIOT_COEFF * bg
        shear2 = w.at(mat, U)
        shear1 = 0.5 * shear2
        for i, e in enumerate((exx, ezz, eyy)):
            w.put(st, SXX + i, w.at(st, SXX + i) + (shear2 * e + bulk))
        for i, e in enumerate((gxz, gxy, gzy)):
            w.put(st, SXZ + i, w.at(st, SXZ + i) + shear1 * e)
        w.put(st, PR, add_source(w, 0, w.at(st, PR) - bg))
        for i, e in enumerate((exx, ezz, eyy, gxz, gxy, gzy, g)):
            e1[i, w.x, w.z0:w.z0 + zc, :] = e

    def turn(w):
        terms = strains(q2, w)
        final = add_source(w, 1, w.at(st, PR) - w.at(mat, B) * terms[7])
        here = slice(w.z0, w.z0 + zc)
        bar_p = w.at(ad, PR) + (cnt[w.x, here, :] * final - obs[w.x, here, :])
        w.put(ad, PR, bar_p)
        parts = correlate(w, [w.at(ad, SXX + i) for i in range(6)], bar_p, terms)
        for k in range(3):
            grad[k, w.x, here, :] = parts[k]

    def back_motion(w):
        vels, fluxes = bar_motion(w)
        damp = w.at(mat, D)
        total = None
        for i in range(3):
            bar_f = C_M * vels[i] - C_B * fluxes[i]
            bar_r = C_A * fluxes[i] - C_B * vels[i]
            w.put(bf, i, bar_f)
            w.put(bf, 3 + i, bar_r)
            part = w.at(q1, i) * bar_r
            total = part if total is None else total + part
            w.put(ad, VX + i, vels[i])
            w.put(ad, QX + i, fluxes[i] - damp * bar_r)
        grad[3, w.x, w.z0:w.z0 + zc, :] = total

    def back_stress(w):
        bars = (
            w.at(ad, SXX) - w.bx(bf, 0),
            w.at(ad, SZZ) - w.bz(bf, 1),
            w.at(ad, SYY) - w.by(bf, 2),
            w.at(ad, SXZ) - (w.fz(bf, 0) + w.fx(bf, 1)),
            w.at(ad, SXY) - (w.fy(bf, 0) + w.fx(bf, 2)),
            w.at(ad, SZY) - (w.fy(bf, 1) + w.fz(bf, 2)))
        bar_p = w.at(ad, PR) + (w.bx(bf, 3) + w.bz(bf, 4) + w.by(bf, 5))
        terms = [rows_of(e1, i, w) for i in range(6)]
        terms += [terms[0] + terms[1] + terms[2], rows_of(e1, 6, w)]
        parts = correlate(w, bars, bar_p, terms)
        for k in range(3):
            grad[k, w.x, w.z0:w.z0 + zc, :] = rows_of(grad, k, w) + parts[k]

    root = float(n) ** 0.5
    signs = (TIME_STEP / root, TIME_STEP / root, TIME_STEP / root, -1.0 / root)

    def finish(w):
        vels, fluxes = bar_motion(w)
        damp = rows_of(grad, 3, w)
        for i in range(3):
            damp = damp + w.at(st, QX + i) * (C_A * fluxes[i] - C_B * vels[i])
        cls = class_ref[w.x, w.z0:w.z0 + zc, :]
        for k in range(4):
            total = damp if k == 3 else rows_of(grad, k, w)
            total = total * (factor_of(k, cls) * signs[k])
            for r in range(0, zc, piece):
                d = (w.z0 + r) // piece
                terms_ref[w.x // per, d // 4, d // 2 % 2, d % 2, k, w.x % per] = total[r:r + piece]

    stages = (
        functools.partial(velocities, st, QX, q1), stresses, functools.partial(velocities, q1, 0, q2),
        turn, back_motion, back_stress, finish)
    fwd_copy(0).wait()

    def plane_step(c, j):
        t = c * per + j

        @pl.when(t + 1 < planes)
        def _():
            fwd_copy(t + 1).wait()

        @pl.when(t < planes)
        def _():
            build_plane(c, j, t)

        for s, stage in enumerate(stages):
            x = t - s

            @pl.when(jnp.logical_and(x >= 0, x < planes))
            def _():
                if s == 3:
                    adj_copy(x).wait()
                for z0 in range(0, nz, zc):
                    stage(Window(x, z0, zc, nz, ny))

    def chunk_step(c, carry):
        within(c + 3, gather_0)
        within(c + 2, gather_1)
        within(c + 1, gather_2)
        within(c, gather_3)

        def inner(j, inner_carry):
            plane_step(c, j)
            return inner_carry

        lax.fori_loop(0, per, inner, 0)
        done = c - lag
        within(done, reduce_0)
        within(done - 1, reduce_1)
        within(done - 2, reduce_2)
        within(done - 3, reduce_3)
        return carry

    lax.fori_loop(0, chunks + lag, chunk_step, 0)
    last = chunks - 1
    reduce_1(last)
    if last >= 1:
        reduce_2(last - 1)
    reduce_2(last)
    for c in range(max(0, last - 2), chunks):
        reduce_3(c)

    def settle(c, carry):
        for d in range(1, zs):
            gather_line(c, d).wait_send()
            reduce_line(c, d).wait_send()
        for copy in (gather_side(c), gather_core(c), reduce_core(c), reduce_side(c)):
            copy.wait_send()
        return carry

    lax.fori_loop(0, chunks, settle, 0)


def per_device(forward_state, adjoint_state, source_amp, source_cell, receiver_cells, recorded, material,
               cell_class, class_factors):
    n = lax.axis_size("shot")
    params, planes, piece, ny = material.shape
    fields, _, nz, _ = forward_state.shape[1:]
    per = 2 if planes % 2 == 0 else 1
    chunks, zs = planes // per, n // 4
    block = (params, per, piece, ny)
    hbm = pl.BlockSpec(memory_space=pltpu.HBM)
    vmem = lambda *shape: pltpu.VMEM(shape, F32)
    padded = lambda f: vmem(f, planes + 2, nz, ny)
    plain = lambda f: vmem(f, planes, nz, ny)
    dma = pltpu.SemaphoreType.DMA
    return pl.pallas_call(
        functools.partial(kernel, n, 8),
        out_shape=jax.ShapeDtypeStruct(material.shape, F32),
        in_specs=[hbm] * 9,
        out_specs=pl.BlockSpec(memory_space=pltpu.VMEM),
        scratch_shapes=[
            pltpu.SMEM(source_amp.shape, F32), pltpu.SMEM(source_cell.shape, jnp.int32),
            pltpu.VMEM(receiver_cells.shape, jnp.int32), pltpu.VMEM(recorded.shape, F32),
            pltpu.VMEM(cell_class.shape, jnp.int32), pltpu.SMEM(class_factors.shape, F32),
            vmem(chunks, zs, 2, 2, *block), vmem(chunks, zs, 2, 2, *block),
            vmem(chunks, zs, 2, *block), vmem(chunks, zs, *block), vmem(chunks, zs, *block),
            vmem(chunks, zs - 1, *block), vmem(chunks, zs - 1, *block),
            padded(fields), padded(fields), padded(3), padded(3), plain(7), padded(7), padded(6), padded(4), plain(4),
            vmem(planes, nz, ny), vmem(planes, nz, ny),
            dma((planes,)), dma((planes,)), dma((6,)), dma((chunks,)),
            dma((zs - 1, chunks)), dma((zs - 1, chunks)), dma((chunks,)), dma((chunks,)), dma((chunks,)), dma((chunks,)),
            dma((chunks,)), dma((chunks,)), dma((chunks,)), dma((chunks,)), dma((zs - 1, chunks)), dma((zs - 1, chunks))],
        compiler_params=pltpu.CompilerParams(
            collective_id=0, has_side_effects=True, vmem_limit_bytes=60 << 20),
        name="gradient",
    )(forward_state[0], adjoint_state[0], source_amp, source_cell, receiver_cells, recorded, material,
      cell_class, class_factors)


def solution(mesh):
    placed = (
        P(("groups", "shot"), None, None, None, None),
        P(("groups", "shot"), None, None, None, None),
        P(("groups", "shot"), None),
        P(("groups", "shot")),
        P(("groups", "shot"), None),
        P(("groups", "shot"), None),
        P(None, "groups", "shot", None),
        P("groups", None, None),
        P(),
    )
    return jax.shard_map(
        per_device, mesh=mesh, in_specs=placed, out_specs=P(None, "groups", "shot", None), check_vma=False)
```

```python
import functools

import jax
import jax.numpy as jnp
from jax import lax
from jax.experimental import pallas as pl
from jax.experimental.pallas import tpu as pltpu
from jax.sharding import PartitionSpec as P

BIOT_COEFF = 0.8
RHO_BULK = 2.2
RHO_FLUID = 1.0
MASS_FLUID = 2.5
TIME_STEP = 0.25
DET = RHO_BULK * MASS_FLUID - RHO_FLUID * RHO_FLUID
C_M = TIME_STEP * MASS_FLUID / DET
C_A = TIME_STEP * RHO_BULK / DET
C_B = TIME_STEP * RHO_FLUID / DET

VX, VZ, VY, QX, QZ, QY, SXX, SZZ, SYY, SXZ, SXY, SZY, PR = range(13)
MESH = pl.DeviceIdType.MESH
F32 = jnp.float32


def coordinates(n):
    me = lax.axis_index("shot")
    return lax.rem(me, 2), lax.rem(me // 2, 2), me // 4, n // 4


def index_of(z, y, core):
    return (z * 2 + y) * 2 + core


class Window:
    def __init__(self, x, z0, zc, nz, ny):
        self.x, self.z0, self.zc, self.nz = x, z0, zc, nz
        self.row = lax.broadcasted_iota(jnp.int32, (zc, ny), 0)
        self.lane = lax.broadcasted_iota(jnp.int32, (zc, ny), 1)
        self.ny = ny
        self.seen = {}

    def at(self, ref, f, dx=0, dz=0):
        key = (id(ref), f, dx, dz)
        if key in self.seen:
            return self.seen[key]
        plane = self.x + 1 + dx
        lo = self.z0 + dz
        if lo < 0:
            value = self.at(ref, f, dx)
            value = jnp.where(self.row == 0, 0.0, pltpu.roll(value, 1, 0))
        elif lo + self.zc > self.nz:
            value = self.at(ref, f, dx)
            value = jnp.where(self.row == self.zc - 1, 0.0, pltpu.roll(value, self.zc - 1, 0))
        else:
            value = ref[f, plane, lo:lo + self.zc, :]
        self.seen[key] = value
        return value

    def fx(self, ref, f):
        return self.at(ref, f, 1) - self.at(ref, f)

    def bx(self, ref, f):
        return self.at(ref, f) - self.at(ref, f, -1)

    def fz(self, ref, f):
        return self.at(ref, f, 0, 1) - self.at(ref, f)

    def bz(self, ref, f):
        return self.at(ref, f) - self.at(ref, f, 0, -1)

    def fy(self, ref, f):
        value = self.at(ref, f)
        return jnp.where(self.lane == self.ny - 1, 0.0, pltpu.roll(value, self.ny - 1, 1)) - value

    def by(self, ref, f):
        value = self.at(ref, f)
        return value - jnp.where(self.lane == 0, 0.0, pltpu.roll(value, 1, 1))

    def put(self, ref, f, value):
        ref[f, self.x + 1, self.z0:self.z0 + self.zc, :] = value


STAGES = 7
GATHER_LEAD = (6, 3, 1)
REDUCE_LAG = (1, 3, 5)


def kernel(n, zc, fwd_hbm, adj_hbm, amp_hbm, src_hbm, rec_hbm, obs_hbm, own_hbm, class_hbm, cf_hbm,
           out_ref, amp_ref, src_ref, rec_ref, obs_in, class_ref, cf_ref, gathered, terms_ref,
           from_core, to_side, from_side, to_line, from_line,
           st, ad, q1, q2, e1, be, bf, mat, grad, cnt, obs,
           fwd_sem, adj_sem, small_sem, own_sem,
           gz_s, gz_r, gy_s, gy_r, gc_s, gc_r, rc_s, rc_r, ry_s, ry_r, rz_s, rz_r):
    planes, nz, ny = class_ref.shape
    chunks, zs = gathered.shape[0], gathered.shape[1]
    per = planes // chunks
    lag = -(-(STAGES - 1) // per)
    piece = gathered.shape[6]
    classes = cf_ref.shape[1]
    core, y, z, _ = coordinates(n)
    other_core = {"shot": index_of(z, y, 1 - core)}
    other_side = {"shot": index_of(z, 1 - y, core)}

    def on_line(d):
        return lax.rem(z + d, zs)

    def own_copy(c):
        return pltpu.make_async_copy(own_hbm.at[:, pl.ds(c * per, per)], gathered.at[c, z, y, core], own_sem.at[c])

    def fwd_copy(x):
        return pltpu.make_async_copy(fwd_hbm.at[:, x], st.at[:, x + 1], fwd_sem.at[x])

    def adj_copy(x):
        return pltpu.make_async_copy(adj_hbm.at[:, x], ad.at[:, x + 1], adj_sem.at[x])

    small = [pltpu.make_async_copy(src, dst, small_sem.at[i]) for i, (src, dst) in enumerate((
        (rec_hbm, rec_ref), (obs_hbm, obs_in), (amp_hbm, amp_ref), (src_hbm, src_ref), (cf_hbm, cf_ref),
        (class_hbm, class_ref)))]

    def remote(src, dst, send_sem, recv_sem, target):
        return pltpu.make_async_remote_copy(
            src_ref=src, dst_ref=dst, send_sem=send_sem, recv_sem=recv_sem, device_id=target, device_id_type=MESH)

    def gather_line(c, d):
        slab = gathered.at[c, z, y, core]
        return remote(slab, slab, gz_s.at[d - 1, c], gz_r.at[d - 1, c], {"shot": index_of(on_line(d), y, core)})

    def gather_side(c):
        slabs = gathered.at[c, :, y, core]
        return remote(slabs, slabs, gy_s.at[c], gy_r.at[c], other_side)

    def gather_core(c):
        slabs = gathered.at[c, :, :, core]
        return remote(slabs, slabs, gc_s.at[c], gc_r.at[c], other_core)

    def reduce_core(c):
        return remote(terms_ref.at[c, :, :, 1 - core], from_core.at[c], rc_s.at[c], rc_r.at[c], other_core)

    def reduce_side(c):
        return remote(to_side.at[c], from_side.at[c], ry_s.at[c], ry_r.at[c], other_side)

    def reduce_line(c, d):
        return remote(to_line.at[c, d - 1], from_line.at[c, d - 1], rz_s.at[d - 1, c], rz_r.at[d - 1, c],
                      {"shot": index_of(on_line(d), y, core)})

    def within(c, step):
        @pl.when(jnp.logical_and(c >= 0, c < chunks))
        def _():
            step(c)

    def gather_0(c):
        own_copy(c).wait()
        for d in range(1, zs):
            gather_line(c, d).start()

    def gather_1(c):
        for d in range(1, zs):
            gather_line(c, d).wait_recv()
        gather_side(c).start()

    def gather_2(c):
        gather_side(c).wait_recv()
        gather_core(c).start()

    def gather_3(c):
        gather_core(c).wait_recv()

    def reduce_0(c):
        reduce_core(c).start()

    def reduce_1(c):
        reduce_core(c).wait_recv()
        for s in range(zs):
            to_side[c, s] = terms_ref[c, s, 1 - y, core] + from_core[c, s, 1 - y]
        reduce_side(c).start()

    def reduce_2(c):
        reduce_side(c).wait_recv()
        for d in range(1, zs):
            s = on_line(d)
            to_line[c, d - 1] = terms_ref[c, s, y, core] + from_core[c, s, y] + from_side[c, s]
            reduce_line(c, d).start()

    def reduce_3(c):
        total = terms_ref[c, z, y, core] + from_core[c, z, y] + from_side[c, z]
        for d in range(1, zs):
            reduce_line(c, d).wait_recv()
            total = total + from_line[c, d - 1]
        out_ref[:, pl.ds(c * per, per)] = total

    for c in range(chunks):
        own_copy(c).start()
    for copy in small:
        copy.start()
    for x in range(planes):
        fwd_copy(x).start()
    for x in range(planes):
        adj_copy(x).start()

    barrier = pltpu.get_barrier_semaphore()
    for target in [other_core, other_side] + [{"shot": index_of(on_line(d), y, core)} for d in range(1, zs)]:
        pl.semaphore_signal(barrier, inc=1, device_id=target, device_id_type=MESH)
    zero_plane = jnp.zeros((nz, ny), F32)
    for ref in (st, q1, q2, be, bf):
        for f in range(ref.shape[0]):
            ref[f, 0] = zero_plane
            ref[f, planes + 1] = zero_plane
    pl.semaphore_wait(barrier, zs + 1)

    gathers = (gather_0, gather_1, gather_2)

    def lead_in(first, last):
        for v in range(first, last):
            for step, lead in zip(gathers, GATHER_LEAD):
                if 0 <= v + lead < chunks:
                    step(v + lead)

    lead_in(-GATHER_LEAD[0], -GATHER_LEAD[1])
    for copy in small:
        copy.wait()

    cells = rec_ref[...]
    rows = lax.div(cells, jnp.int32(ny))
    lanes = cells - rows * ny
    count = cells.shape[1]
    value = obs_in[...]
    hi = value.astype(jnp.bfloat16).astype(F32)
    mid = (value - hi).astype(jnp.bfloat16).astype(F32)
    low = value - hi - mid
    hit = lax.broadcasted_iota(jnp.int32, (ny, count), 0) == lanes
    columns = jnp.concatenate(
        [jnp.where(hit, part, 0.0).astype(jnp.bfloat16) for part in (jnp.ones_like(value), hi, mid, low)], axis=0)

    group = 4 if planes % 4 == 0 else 1

    def place_receivers(g, carry):
        at_row = lax.broadcasted_iota(jnp.int32, (group * nz, count), 0) + g * (group * nz) == rows
        product = lax.dot_general(
            jnp.where(at_row, 1.0, 0.0).astype(jnp.bfloat16), columns, (((1,), (1,)), ((), ())),
            preferred_element_type=F32)
        here = pl.ds(g * group, group)
        cnt[here] = product[:, :ny].reshape(group, nz, ny)
        seen = product[:, ny:2 * ny] + product[:, 2 * ny:3 * ny] + product[:, 3 * ny:]
        obs[here] = seen.reshape(group, nz, ny)
        return carry

    lax.fori_loop(0, planes // group, place_receivers, 0)
    lead_in(-GATHER_LEAD[1], 0)

    def factor_of(k, cls):
        factor = jnp.full(cls.shape, cf_ref[k, classes - 1], F32)
        for c in range(classes - 1):
            factor = jnp.where(cls == c, cf_ref[k, c], factor)
        return factor

    scales = (TIME_STEP, 2.0 * TIME_STEP, TIME_STEP, 1.0)

    source = src_ref[0]
    L, U, B, D = range(4)

    def velocities(q_old, base, q_new, w):
        damp = w.at(mat, D)
        forces = (
            w.fx(st, SXX) + w.bz(st, SXZ) + w.by(st, SXY),
            w.bx(st, SXZ) + w.fz(st, SZZ) + w.by(st, SZY),
            w.bx(st, SXY) + w.bz(st, SZY) + w.fy(st, SYY))
        slopes = (w.fx(st, PR), w.fz(st, PR), w.fy(st, PR))
        for i in range(3):
            flux = w.at(q_old, base + i)
            pull = slopes[i] + damp * flux
            w.put(st, VX + i, w.at(st, VX + i) + (C_M * forces[i] + C_B * pull))
            w.put(q_new, i, flux - (C_A * pull + C_B * forces[i]))

    def strains(q, w):
        exx, ezz, eyy = w.bx(st, VX), w.bz(st, VZ), w.by(st, VY)
        dv = exx + ezz + eyy
        g = BIOT_COEFF * dv + (w.bx(q, 0) + w.bz(q, 1) + w.by(q, 2))
        gxz = w.fz(st, VX) + w.fx(st, VZ)
        gxy = w.fy(st, VX) + w.fx(st, VY)
        gzy = w.fy(st, VZ) + w.fz(st, VY)
        return exx, ezz, eyy, gxz, gxy, gzy, dv, g

    def add_source(w, section, pressure):
        here = (w.row + (w.x * nz + w.z0)) * ny + w.lane == source
        return pressure + jnp.where(here, amp_ref[0, section], 0.0)

    def correlate(w, bars, bar_p, terms):
        exx, ezz, eyy, gxz, gxy, gzy, dv, g = terms
        trace = bars[0] + bars[1] + bars[2]
        aside = BIOT_COEFF * trace - bar_p
        g_lame = trace * dv
        g_shear = 2.0 * (bars[0] * exx + bars[1] * ezz + bars[2] * eyy) + (
            bars[3] * gxz + bars[4] * gxy + bars[5] * gzy)
        g_biot = g * aside
        h = w.at(mat, B) * aside
        common = w.at(mat, L) * trace + BIOT_COEFF * h
        shear2 = w.at(mat, U)
        shear1 = 0.5 * shear2
        for i in range(3):
            w.put(be, i, shear2 * bars[i] + common)
            w.put(be, 3 + i, shear1 * bars[3 + i])
        w.put(be, 6, h)
        return g_lame, g_shear, g_biot

    def bar_motion(w):
        vels = (
            w.at(ad, VX) - (w.fx(be, 0) + w.bz(be, 3) + w.by(be, 4)),
            w.at(ad, VZ) - (w.fz(be, 1) + w.bx(be, 3) + w.by(be, 5)),
            w.at(ad, VY) - (w.fy(be, 2) + w.bx(be, 4) + w.bz(be, 5)))
        fluxes = (
            w.at(ad, QX) - w.fx(be, 6), w.at(ad, QZ) - w.fz(be, 6), w.at(ad, QY) - w.fy(be, 6))
        return vels, fluxes

    def rows_of(ref, k, w):
        return ref[k, w.x, w.z0:w.z0 + zc, :]


    def build_plane(c, j, x):
        cls = class_ref[x]
        for k in range(4):
            for d in range(n):
                mat[k, x + 1, d * piece:(d + 1) * piece, :] = gathered[c, d // 4, d // 2 % 2, d % 2, k, j]
            mat[k, x + 1] = mat[k, x + 1] * factor_of(k, cls) * scales[k]

    def stresses(w):
        terms = strains(q1, w)
        exx, ezz, eyy, gxz, gxy, gzy, dv, g = terms
        bg = w.at(mat, B) * g
        bulk = w.at(mat, L) * dv + BIOT_COEFF * bg
        shear2 = w.at(mat, U)
        shear1 = 0.5 * shear2
        for i, e in enumerate((exx, ezz, eyy)):
            w.put(st, SXX + i, w.at(st, SXX + i) + (shear2 * e + bulk))
        for i, e in enumerate((gxz, gxy, gzy)):
            w.put(st, SXZ + i, w.at(st, SXZ + i) + shear1 * e)
        w.put(st, PR, add_source(w, 0, w.at(st, PR) - bg))
        for i, e in enumerate((exx, ezz, eyy, gxz, gxy, gzy, g)):
            e1[i, w.x, w.z0:w.z0 + zc, :] = e

    def turn(w):
        terms = strains(q2, w)
        final = add_source(w, 1, w.at(st, PR) - w.at(mat, B) * terms[7])
        here = slice(w.z0, w.z0 + zc)
        bar_p = w.at(ad, PR) + (cnt[w.x, here, :] * final - obs[w.x, here, :])
        w.put(ad, PR, bar_p)
        parts = correlate(w, [w.at(ad, SXX + i) for i in range(6)], bar_p, terms)
        for k in range(3):
            grad[k, w.x, here, :] = parts[k]

    def back_motion(w):
        vels, fluxes = bar_motion(w)
        damp = w.at(mat, D)
        total = None
        for i in range(3):
            bar_f = C_M * vels[i] - C_B * fluxes[i]
            bar_r = C_A * fluxes[i] - C_B * vels[i]
            w.put(bf, i, bar_f)
            w.put(bf, 3 + i, bar_r)
            part = w.at(q1, i) * bar_r
            total = part if total is None else total + part
            w.put(ad, VX + i, vels[i])
            w.put(ad, QX + i, fluxes[i] - damp * bar_r)
        grad[3, w.x, w.z0:w.z0 + zc, :] = total

    def back_stress(w):
        bars = (
            w.at(ad, SXX) - w.bx(bf, 0),
            w.at(ad, SZZ) - w.bz(bf, 1),
            w.at(ad, SYY) - w.by(bf, 2),
            w.at(ad, SXZ) - (w.fz(bf, 0) + w.fx(bf, 1)),
            w.at(ad, SXY) - (w.fy(bf, 0) + w.fx(bf, 2)),
            w.at(ad, SZY) - (w.fy(bf, 1) + w.fz(bf, 2)))
        bar_p = w.at(ad, PR) + (w.bx(bf, 3) + w.bz(bf, 4) + w.by(bf, 5))
        terms = [rows_of(e1, i, w) for i in range(6)]
        terms += [terms[0] + terms[1] + terms[2], rows_of(e1, 6, w)]
        parts = correlate(w, bars, bar_p, terms)
        for k in range(3):
            grad[k, w.x, w.z0:w.z0 + zc, :] = rows_of(grad, k, w) + parts[k]

    root = float(n) ** 0.5
    signs = (TIME_STEP / root, TIME_STEP / root, TIME_STEP / root, -1.0 / root)

    def finish(w):
        vels, fluxes = bar_motion(w)
        damp = rows_of(grad, 3, w)
        for i in range(3):
            damp = damp + w.at(st, QX + i) * (C_A * fluxes[i] - C_B * vels[i])
        cls = class_ref[w.x, w.z0:w.z0 + zc, :]
        for k in range(4):
            total = damp if k == 3 else rows_of(grad, k, w)
            total = total * (factor_of(k, cls) * signs[k])
            for r in range(0, zc, piece):
                d = (w.z0 + r) // piece
                terms_ref[w.x // per, d // 4, d // 2 % 2, d % 2, k, w.x % per] = total[r:r + piece]

    stages = (
        functools.partial(velocities, st, QX, q1), stresses, functools.partial(velocities, q1, 0, q2),
        turn, back_motion, back_stress, finish)
    fwd_copy(0).wait()

    def plane_step(c, j):
        t = c * per + j

        @pl.when(t + 1 < planes)
        def _():
            fwd_copy(t + 1).wait()

        @pl.when(t < planes)
        def _():
            build_plane(c, j, t)

        for s, stage in enumerate(stages):
            x = t - s

            @pl.when(jnp.logical_and(x >= 0, x < planes))
            def _():
                if s == 3:
                    adj_copy(x).wait()
                for z0 in range(0, nz, zc):
                    stage(Window(x, z0, zc, nz, ny))

    reduces = (reduce_1, reduce_2, reduce_3)

    def chunk_step(c, carry):
        for step, lead in zip(gathers, GATHER_LEAD):
            within(c + lead, step)
        within(c, gather_3)

        def inner(j, inner_carry):
            plane_step(c, j)
            return inner_carry

        lax.fori_loop(0, per, inner, 0)
        done = c - lag
        within(done, reduce_0)
        for step, behind in zip(reduces, REDUCE_LAG):
            within(done - behind, step)
        return carry

    lax.fori_loop(0, chunks + lag, chunk_step, 0)
    for v in range(chunks, chunks + REDUCE_LAG[2]):
        for step, behind in zip(reduces, REDUCE_LAG):
            if 0 <= v - behind < chunks:
                step(v - behind)

    def settle(c, carry):
        for d in range(1, zs):
            gather_line(c, d).wait_send()
            reduce_line(c, d).wait_send()
        for copy in (gather_side(c), gather_core(c), reduce_core(c), reduce_side(c)):
            copy.wait_send()
        return carry

    lax.fori_loop(0, chunks, settle, 0)


def per_device(forward_state, adjoint_state, source_amp, source_cell, receiver_cells, recorded, material,
               cell_class, class_factors):
    n = lax.axis_size("shot")
    params, planes, piece, ny = material.shape
    fields, _, nz, _ = forward_state.shape[1:]
    per = 2 if planes % 2 == 0 else 1
    chunks, zs = planes // per, n // 4
    block = (params, per, piece, ny)
    hbm = pl.BlockSpec(memory_space=pltpu.HBM)
    vmem = lambda *shape: pltpu.VMEM(shape, F32)
    padded = lambda f: vmem(f, planes + 2, nz, ny)
    plain = lambda f: vmem(f, planes, nz, ny)
    dma = pltpu.SemaphoreType.DMA
    return pl.pallas_call(
        functools.partial(kernel, n, 8),
        out_shape=jax.ShapeDtypeStruct(material.shape, F32),
        in_specs=[hbm] * 9,
        out_specs=pl.BlockSpec(memory_space=pltpu.VMEM),
        scratch_shapes=[
            pltpu.SMEM(source_amp.shape, F32), pltpu.SMEM(source_cell.shape, jnp.int32),
            pltpu.VMEM(receiver_cells.shape, jnp.int32), pltpu.VMEM(recorded.shape, F32),
            pltpu.VMEM(cell_class.shape, jnp.int32), pltpu.SMEM(class_factors.shape, F32),
            vmem(chunks, zs, 2, 2, *block), vmem(chunks, zs, 2, 2, *block),
            vmem(chunks, zs, 2, *block), vmem(chunks, zs, *block), vmem(chunks, zs, *block),
            vmem(chunks, zs - 1, *block), vmem(chunks, zs - 1, *block),
            padded(fields), padded(fields), padded(3), padded(3), plain(7), padded(7), padded(6), padded(4), plain(4),
            vmem(planes, nz, ny), vmem(planes, nz, ny),
            dma((planes,)), dma((planes,)), dma((6,)), dma((chunks,)),
            dma((zs - 1, chunks)), dma((zs - 1, chunks)), dma((chunks,)), dma((chunks,)), dma((chunks,)), dma((chunks,)),
            dma((chunks,)), dma((chunks,)), dma((chunks,)), dma((chunks,)), dma((zs - 1, chunks)), dma((zs - 1, chunks))],
        compiler_params=pltpu.CompilerParams(
            collective_id=0, has_side_effects=True, vmem_limit_bytes=60 << 20),
        name="gradient",
    )(forward_state[0], adjoint_state[0], source_amp, source_cell, receiver_cells, recorded, material,
      cell_class, class_factors)


def solution(mesh):
    placed = (
        P(("groups", "shot"), None, None, None, None),
        P(("groups", "shot"), None, None, None, None),
        P(("groups", "shot"), None),
        P(("groups", "shot")),
        P(("groups", "shot"), None),
        P(("groups", "shot"), None),
        P(None, "groups", "shot", None),
        P("groups", None, None),
        P(),
    )
    return jax.shard_map(
        per_device, mesh=mesh, in_specs=placed, out_specs=P(None, "groups", "shot", None), check_vma=False)
```

```python
import functools

import jax
import jax.numpy as jnp
from jax import lax
from jax.experimental import pallas as pl
from jax.experimental.pallas import tpu as pltpu
from jax.sharding import PartitionSpec as P

BIOT_COEFF = 0.8
RHO_BULK = 2.2
RHO_FLUID = 1.0
MASS_FLUID = 2.5
TIME_STEP = 0.25
DET = RHO_BULK * MASS_FLUID - RHO_FLUID * RHO_FLUID
C_M = TIME_STEP * MASS_FLUID / DET
C_A = TIME_STEP * RHO_BULK / DET
C_B = TIME_STEP * RHO_FLUID / DET

VX, VZ, VY, QX, QZ, QY, SXX, SZZ, SYY, SXZ, SXY, SZY, PR = range(13)
MESH = pl.DeviceIdType.MESH
F32 = jnp.float32


def coordinates(n):
    me = lax.axis_index("shot")
    return lax.rem(me, 2), lax.rem(me // 2, 2), me // 4, n // 4


def index_of(z, y, core):
    return (z * 2 + y) * 2 + core


class Window:
    def __init__(self, x, z0, zc, nz, ny):
        self.x, self.z0, self.zc, self.nz = x, z0, zc, nz
        self.row = lax.broadcasted_iota(jnp.int32, (zc, ny), 0)
        self.lane = lax.broadcasted_iota(jnp.int32, (zc, ny), 1)
        self.ny = ny
        self.seen = {}

    def at(self, ref, f, dx=0, dz=0):
        key = (id(ref), f, dx, dz)
        if key in self.seen:
            return self.seen[key]
        plane = self.x + 1 + dx
        lo = self.z0 + dz
        if lo < 0:
            value = self.at(ref, f, dx)
            value = jnp.where(self.row == 0, 0.0, pltpu.roll(value, 1, 0))
        elif lo + self.zc > self.nz:
            value = self.at(ref, f, dx)
            value = jnp.where(self.row == self.zc - 1, 0.0, pltpu.roll(value, self.zc - 1, 0))
        else:
            value = ref[f, plane, lo:lo + self.zc, :]
        self.seen[key] = value
        return value

    def fx(self, ref, f):
        return self.at(ref, f, 1) - self.at(ref, f)

    def bx(self, ref, f):
        return self.at(ref, f) - self.at(ref, f, -1)

    def fz(self, ref, f):
        return self.at(ref, f, 0, 1) - self.at(ref, f)

    def bz(self, ref, f):
        return self.at(ref, f) - self.at(ref, f, 0, -1)

    def fy(self, ref, f):
        value = self.at(ref, f)
        return jnp.where(self.lane == self.ny - 1, 0.0, pltpu.roll(value, self.ny - 1, 1)) - value

    def by(self, ref, f):
        value = self.at(ref, f)
        return value - jnp.where(self.lane == 0, 0.0, pltpu.roll(value, 1, 1))

    def put(self, ref, f, value):
        ref[f, self.x + 1, self.z0:self.z0 + self.zc, :] = value


STAGES = 7
GATHER_LEAD = (6, 3, 1)
REDUCE_LAG = (1, 3, 5)


def kernel(n, zc, fwd_hbm, adj_hbm, amp_hbm, src_hbm, rec_hbm, obs_hbm, own_hbm, class_hbm, cf_hbm,
           out_ref, amp_ref, src_ref, rec_ref, obs_in, class_ref, cf_ref, gathered, terms_ref,
           from_core, to_side, from_side, to_line, from_line,
           st, ad, q1, q2, e1, be, bf, mat, grad, cnt, obs,
           fwd_sem, adj_sem, small_sem, own_sem,
           gz_s, gz_r, gy_s, gy_r, gc_s, gc_r, rc_s, rc_r, ry_s, ry_r, rz_s, rz_r):
    planes, nz, ny = class_ref.shape
    chunks, zs = gathered.shape[0], gathered.shape[1]
    per = planes // chunks
    lag = -(-(STAGES - 1) // per)
    piece = gathered.shape[6]
    classes = cf_ref.shape[1]
    core, y, z, _ = coordinates(n)
    other_core = {"shot": index_of(z, y, 1 - core)}
    other_side = {"shot": index_of(z, 1 - y, core)}

    def on_line(d):
        return lax.rem(z + d, zs)

    def own_copy(c):
        return pltpu.make_async_copy(own_hbm.at[:, pl.ds(c * per, per)], gathered.at[c, z, y, core], own_sem.at[c])

    def fwd_copy(x):
        return pltpu.make_async_copy(fwd_hbm.at[:, x], st.at[:, x + 1], fwd_sem.at[x])

    def adj_copy(x):
        return pltpu.make_async_copy(adj_hbm.at[:, x], ad.at[:, x + 1], adj_sem.at[x])

    small = [pltpu.make_async_copy(src, dst, small_sem.at[i]) for i, (src, dst) in enumerate((
        (rec_hbm, rec_ref), (obs_hbm, obs_in), (amp_hbm, amp_ref), (src_hbm, src_ref), (cf_hbm, cf_ref),
        (class_hbm, class_ref)))]

    def remote(src, dst, send_sem, recv_sem, target):
        return pltpu.make_async_remote_copy(
            src_ref=src, dst_ref=dst, send_sem=send_sem, recv_sem=recv_sem, device_id=target, device_id_type=MESH)

    def gather_line(c, d):
        slab = gathered.at[c, z, y, core]
        return remote(slab, slab, gz_s.at[d - 1, c], gz_r.at[d - 1, c], {"shot": index_of(on_line(d), y, core)})

    def gather_side(c):
        slabs = gathered.at[c, :, y, core]
        return remote(slabs, slabs, gy_s.at[c], gy_r.at[c], other_side)

    def gather_core(c):
        slabs = gathered.at[c, :, :, core]
        return remote(slabs, slabs, gc_s.at[c], gc_r.at[c], other_core)

    def reduce_core(c):
        return remote(terms_ref.at[c, :, :, 1 - core], from_core.at[c], rc_s.at[c], rc_r.at[c], other_core)

    def reduce_side(c):
        return remote(to_side.at[c], from_side.at[c], ry_s.at[c], ry_r.at[c], other_side)

    def reduce_line(c, d):
        return remote(to_line.at[c, d - 1], from_line.at[c, d - 1], rz_s.at[d - 1, c], rz_r.at[d - 1, c],
                      {"shot": index_of(on_line(d), y, core)})

    def within(c, step):
        @pl.when(jnp.logical_and(c >= 0, c < chunks))
        def _():
            step(c)

    def gather_0(c):
        own_copy(c).wait()
        for d in range(1, zs):
            gather_line(c, d).start()

    def gather_1(c):
        for d in range(1, zs):
            gather_line(c, d).wait_recv()
        gather_side(c).start()

    def gather_2(c):
        gather_side(c).wait_recv()
        gather_core(c).start()

    def gather_3(c):
        gather_core(c).wait_recv()

    def reduce_0(c):
        reduce_core(c).start()

    def reduce_1(c):
        reduce_core(c).wait_recv()
        for s in range(zs):
            to_side[c, s] = terms_ref[c, s, 1 - y, core] + from_core[c, s, 1 - y]
        reduce_side(c).start()

    def reduce_2(c):
        reduce_side(c).wait_recv()
        for d in range(1, zs):
            s = on_line(d)
            to_line[c, d - 1] = terms_ref[c, s, y, core] + from_core[c, s, y] + from_side[c, s]
            reduce_line(c, d).start()

    def reduce_3(c):
        total = terms_ref[c, z, y, core] + from_core[c, z, y] + from_side[c, z]
        for d in range(1, zs):
            reduce_line(c, d).wait_recv()
            total = total + from_line[c, d - 1]
        out_ref[:, pl.ds(c * per, per)] = total

    for c in range(chunks):
        own_copy(c).start()
    for copy in small:
        copy.start()
    for x in range(planes):
        fwd_copy(x).start()
    for x in range(planes):
        adj_copy(x).start()

    barrier = pltpu.get_barrier_semaphore()
    for target in [other_core, other_side] + [{"shot": index_of(on_line(d), y, core)} for d in range(1, zs)]:
        pl.semaphore_signal(barrier, inc=1, device_id=target, device_id_type=MESH)
    zero_plane = jnp.zeros((nz, ny), F32)
    for ref in (st, q1, q2, be, bf):
        for f in range(ref.shape[0]):
            ref[f, 0] = zero_plane
            ref[f, planes + 1] = zero_plane
    pl.semaphore_wait(barrier, zs + 1)

    gathers = (gather_0, gather_1, gather_2)

    def lead_in(first, last):
        for v in range(first, last):
            for step, lead in zip(gathers, GATHER_LEAD):
                if 0 <= v + lead < chunks:
                    step(v + lead)

    lead_in(-GATHER_LEAD[0], -GATHER_LEAD[1])
    for copy in small:
        copy.wait()

    cells = rec_ref[...]
    rows = lax.div(cells, jnp.int32(ny))
    lanes = cells - rows * ny
    count = cells.shape[1]
    value = obs_in[...]
    hi = value.astype(jnp.bfloat16).astype(F32)
    mid = (value - hi).astype(jnp.bfloat16).astype(F32)
    low = value - hi - mid
    hit = lax.broadcasted_iota(jnp.int32, (ny, count), 0) == lanes
    columns = jnp.concatenate(
        [jnp.where(hit, part, 0.0).astype(jnp.bfloat16) for part in (jnp.ones_like(value), hi, mid, low)], axis=0)

    group = 4 if planes % 4 == 0 else 1

    def place_receivers(g, carry):
        at_row = lax.broadcasted_iota(jnp.int32, (group * nz, count), 0) + g * (group * nz) == rows
        product = lax.dot_general(
            jnp.where(at_row, 1.0, 0.0).astype(jnp.bfloat16), columns, (((1,), (1,)), ((), ())),
            preferred_element_type=F32)
        here = pl.ds(g * group, group)
        cnt[here] = product[:, :ny].reshape(group, nz, ny)
        seen = product[:, ny:2 * ny] + product[:, 2 * ny:3 * ny] + product[:, 3 * ny:]
        obs[here] = seen.reshape(group, nz, ny)
        return carry

    lax.fori_loop(0, planes // group, place_receivers, 0)
    lead_in(-GATHER_LEAD[1], 0)

    def factor_of(k, cls):
        factor = jnp.full(cls.shape, cf_ref[k, classes - 1], F32)
        for c in range(classes - 1):
            factor = jnp.where(cls == c, cf_ref[k, c], factor)
        return factor

    scales = (TIME_STEP, 2.0 * TIME_STEP, TIME_STEP, 1.0)

    source = src_ref[0]
    L, U, B, D = range(4)

    def velocities(q_old, base, q_new, w):
        damp = w.at(mat, D)
        forces = (
            w.fx(st, SXX) + w.bz(st, SXZ) + w.by(st, SXY),
            w.bx(st, SXZ) + w.fz(st, SZZ) + w.by(st, SZY),
            w.bx(st, SXY) + w.bz(st, SZY) + w.fy(st, SYY))
        slopes = (w.fx(st, PR), w.fz(st, PR), w.fy(st, PR))
        for i in range(3):
            flux = w.at(q_old, base + i)
            pull = slopes[i] + damp * flux
            w.put(st, VX + i, w.at(st, VX + i) + (C_M * forces[i] + C_B * pull))
            w.put(q_new, i, flux - (C_A * pull + C_B * forces[i]))

    def strains(q, w):
        exx, ezz, eyy = w.bx(st, VX), w.bz(st, VZ), w.by(st, VY)
        dv = exx + ezz + eyy
        g = BIOT_COEFF * dv + (w.bx(q, 0) + w.bz(q, 1) + w.by(q, 2))
        gxz = w.fz(st, VX) + w.fx(st, VZ)
        gxy = w.fy(st, VX) + w.fx(st, VY)
        gzy = w.fy(st, VZ) + w.fz(st, VY)
        return exx, ezz, eyy, gxz, gxy, gzy, dv, g

    def add_source(w, section, pressure):
        here = (w.row + (w.x * nz + w.z0)) * ny + w.lane == source
        return pressure + jnp.where(here, amp_ref[0, section], 0.0)

    def correlate(w, bars, bar_p, terms):
        exx, ezz, eyy, gxz, gxy, gzy, dv, g = terms
        trace = bars[0] + bars[1] + bars[2]
        aside = BIOT_COEFF * trace - bar_p
        g_lame = trace * dv
        g_shear = 2.0 * (bars[0] * exx + bars[1] * ezz + bars[2] * eyy) + (
            bars[3] * gxz + bars[4] * gxy + bars[5] * gzy)
        g_biot = g * aside
        h = w.at(mat, B) * aside
        common = w.at(mat, L) * trace + BIOT_COEFF * h
        shear2 = w.at(mat, U)
        shear1 = 0.5 * shear2
        for i in range(3):
            w.put(be, i, shear2 * bars[i] + common)
            w.put(be, 3 + i, shear1 * bars[3 + i])
        w.put(be, 6, h)
        return g_lame, g_shear, g_biot

    def bar_motion(w):
        vels = (
            w.at(ad, VX) - (w.fx(be, 0) + w.bz(be, 3) + w.by(be, 4)),
            w.at(ad, VZ) - (w.fz(be, 1) + w.bx(be, 3) + w.by(be, 5)),
            w.at(ad, VY) - (w.fy(be, 2) + w.bx(be, 4) + w.bz(be, 5)))
        fluxes = (
            w.at(ad, QX) - w.fx(be, 6), w.at(ad, QZ) - w.fz(be, 6), w.at(ad, QY) - w.fy(be, 6))
        return vels, fluxes

    def rows_of(ref, k, w):
        return ref[k, w.x, w.z0:w.z0 + zc, :]


    def build_plane(c, j, x):
        cls = class_ref[x]
        for k in range(4):
            for d in range(n):
                mat[k, x + 1, d * piece:(d + 1) * piece, :] = gathered[c, d // 4, d // 2 % 2, d % 2, k, j]
            mat[k, x + 1] = mat[k, x + 1] * factor_of(k, cls) * scales[k]

    def stresses(w):
        terms = strains(q1, w)
        exx, ezz, eyy, gxz, gxy, gzy, dv, g = terms
        bg = w.at(mat, B) * g
        bulk = w.at(mat, L) * dv + BIOT_COEFF * bg
        shear2 = w.at(mat, U)
        shear1 = 0.5 * shear2
        for i, e in enumerate((exx, ezz, eyy)):
            w.put(st, SXX + i, w.at(st, SXX + i) + (shear2 * e + bulk))
        for i, e in enumerate((gxz, gxy, gzy)):
            w.put(st, SXZ + i, w.at(st, SXZ + i) + shear1 * e)
        w.put(st, PR, add_source(w, 0, w.at(st, PR) - bg))
        for i, e in enumerate((exx, ezz, eyy, gxz, gxy, gzy, g)):
            e1[i, w.x, w.z0:w.z0 + zc, :] = e

    def turn(w):
        terms = strains(q2, w)
        final = add_source(w, 1, w.at(st, PR) - w.at(mat, B) * terms[7])
        here = slice(w.z0, w.z0 + zc)
        bar_p = w.at(ad, PR) + (cnt[w.x, here, :] * final - obs[w.x, here, :])
        w.put(ad, PR, bar_p)
        parts = correlate(w, [w.at(ad, SXX + i) for i in range(6)], bar_p, terms)
        for k in range(3):
            grad[k, w.x, here, :] = parts[k]

    def back_motion(w):
        vels, fluxes = bar_motion(w)
        damp = w.at(mat, D)
        total = None
        for i in range(3):
            bar_f = C_M * vels[i] - C_B * fluxes[i]
            bar_r = C_A * fluxes[i] - C_B * vels[i]
            w.put(bf, i, bar_f)
            w.put(bf, 3 + i, bar_r)
            part = w.at(q1, i) * bar_r
            total = part if total is None else total + part
            w.put(ad, VX + i, vels[i])
            w.put(ad, QX + i, fluxes[i] - damp * bar_r)
        grad[3, w.x, w.z0:w.z0 + zc, :] = total

    def back_stress(w):
        bars = (
            w.at(ad, SXX) - w.bx(bf, 0),
            w.at(ad, SZZ) - w.bz(bf, 1),
            w.at(ad, SYY) - w.by(bf, 2),
            w.at(ad, SXZ) - (w.fz(bf, 0) + w.fx(bf, 1)),
            w.at(ad, SXY) - (w.fy(bf, 0) + w.fx(bf, 2)),
            w.at(ad, SZY) - (w.fy(bf, 1) + w.fz(bf, 2)))
        bar_p = w.at(ad, PR) + (w.bx(bf, 3) + w.bz(bf, 4) + w.by(bf, 5))
        terms = [rows_of(e1, i, w) for i in range(6)]
        terms += [terms[0] + terms[1] + terms[2], rows_of(e1, 6, w)]
        parts = correlate(w, bars, bar_p, terms)
        for k in range(3):
            grad[k, w.x, w.z0:w.z0 + zc, :] = rows_of(grad, k, w) + parts[k]

    root = float(n) ** 0.5
    signs = (TIME_STEP / root, TIME_STEP / root, TIME_STEP / root, -1.0 / root)

    def finish(w):
        vels, fluxes = bar_motion(w)
        damp = rows_of(grad, 3, w)
        for i in range(3):
            damp = damp + w.at(st, QX + i) * (C_A * fluxes[i] - C_B * vels[i])
        cls = class_ref[w.x, w.z0:w.z0 + zc, :]
        for k in range(4):
            total = damp if k == 3 else rows_of(grad, k, w)
            total = total * (factor_of(k, cls) * signs[k])
            for r in range(0, zc, piece):
                d = (w.z0 + r) // piece
                terms_ref[w.x // per, d // 4, d // 2 % 2, d % 2, k, w.x % per] = total[r:r + piece]

    stages = (
        functools.partial(velocities, st, QX, q1), stresses, functools.partial(velocities, q1, 0, q2),
        turn, back_motion, back_stress, finish)
    fwd_copy(0).wait()

    def plane_step(c, j):
        t = c * per + j

        @pl.when(t + 1 < planes)
        def _():
            fwd_copy(t + 1).wait()

        @pl.when(t < planes)
        def _():
            build_plane(c, j, t)

        for s, stage in enumerate(stages):
            x = t - s

            @pl.when(jnp.logical_and(x >= 0, x < planes))
            def _():
                if s == 3:
                    adj_copy(x).wait()
                for z0 in range(0, nz, zc):
                    stage(Window(x, z0, zc, nz, ny))

    reduces = (reduce_1, reduce_2, reduce_3)

    def chunk_step(c, carry):
        for step, lead in zip(gathers, GATHER_LEAD):
            within(c + lead, step)
        within(c, gather_3)

        def inner(j, inner_carry):
            plane_step(c, j)
            return inner_carry

        lax.fori_loop(0, per, inner, 0)
        done = c - lag
        within(done, reduce_0)
        for step, behind in zip(reduces, REDUCE_LAG):
            within(done - behind, step)
        return carry

    lax.fori_loop(0, chunks + lag, chunk_step, 0)
    for v in range(chunks, chunks + REDUCE_LAG[2]):
        for step, behind in zip(reduces, REDUCE_LAG):
            if 0 <= v - behind < chunks:
                step(v - behind)

    def settle(c, carry):
        for d in range(1, zs):
            gather_line(c, d).wait_send()
            reduce_line(c, d).wait_send()
        for copy in (gather_side(c), gather_core(c), reduce_core(c), reduce_side(c)):
            copy.wait_send()
        return carry

    lax.fori_loop(0, chunks, settle, 0)


def per_device(forward_state, adjoint_state, source_amp, source_cell, receiver_cells, recorded, material,
               cell_class, class_factors):
    n = lax.axis_size("shot")
    params, planes, piece, ny = material.shape
    fields, _, nz, _ = forward_state.shape[1:]
    per = 2 if planes % 2 == 0 else 1
    chunks, zs = planes // per, n // 4
    block = (params, per, piece, ny)
    hbm = pl.BlockSpec(memory_space=pltpu.HBM)
    vmem = lambda *shape: pltpu.VMEM(shape, F32)
    padded = lambda f: vmem(f, planes + 2, nz, ny)
    plain = lambda f: vmem(f, planes, nz, ny)
    dma = pltpu.SemaphoreType.DMA
    return pl.pallas_call(
        functools.partial(kernel, n, 16),
        out_shape=jax.ShapeDtypeStruct(material.shape, F32),
        in_specs=[hbm] * 9,
        out_specs=pl.BlockSpec(memory_space=pltpu.VMEM),
        scratch_shapes=[
            pltpu.SMEM(source_amp.shape, F32), pltpu.SMEM(source_cell.shape, jnp.int32),
            pltpu.VMEM(receiver_cells.shape, jnp.int32), pltpu.VMEM(recorded.shape, F32),
            pltpu.VMEM(cell_class.shape, jnp.int32), pltpu.SMEM(class_factors.shape, F32),
            vmem(chunks, zs, 2, 2, *block), vmem(chunks, zs, 2, 2, *block),
            vmem(chunks, zs, 2, *block), vmem(chunks, zs, *block), vmem(chunks, zs, *block),
            vmem(chunks, zs - 1, *block), vmem(chunks, zs - 1, *block),
            padded(fields), padded(fields), padded(3), padded(3), plain(7), padded(7), padded(6), padded(4), plain(4),
            vmem(planes, nz, ny), vmem(planes, nz, ny),
            dma((planes,)), dma((planes,)), dma((6,)), dma((chunks,)),
            dma((zs - 1, chunks)), dma((zs - 1, chunks)), dma((chunks,)), dma((chunks,)), dma((chunks,)), dma((chunks,)),
            dma((chunks,)), dma((chunks,)), dma((chunks,)), dma((chunks,)), dma((zs - 1, chunks)), dma((zs - 1, chunks))],
        compiler_params=pltpu.CompilerParams(
            collective_id=0, has_side_effects=True, vmem_limit_bytes=60 << 20),
        name="gradient",
    )(forward_state[0], adjoint_state[0], source_amp, source_cell, receiver_cells, recorded, material,
      cell_class, class_factors)


def solution(mesh):
    placed = (
        P(("groups", "shot"), None, None, None, None),
        P(("groups", "shot"), None, None, None, None),
        P(("groups", "shot"), None),
        P(("groups", "shot")),
        P(("groups", "shot"), None),
        P(("groups", "shot"), None),
        P(None, "groups", "shot", None),
        P("groups", None, None),
        P(),
    )
    return jax.shard_map(
        per_device, mesh=mesh, in_specs=placed, out_specs=P(None, "groups", "shot", None), check_vma=False)
```
